32 devices in a mesh: dp: 16 (over z, y, x), outer: 2 (over core).
Axes of the slice: x: 2, y: 2, z: 4, core: 2. Of those that a mesh axis runs over, the one named last changes fastest.
Arguments:
- latents: bfloat16 [2, 96, 128, 768], P(None, ('dp', 'outer')), may hold values from -6 to 6
- tokens: bfloat16 [2, 41472, 768], P(None, ('dp', 'outer')), may hold values from -6 to 6
- cotangent: bfloat16 [2, 96, 128, 768], P(None, ('dp', 'outer')), may hold values from -6 to 6
- item_count: int32 [2, 32], P(None, ('dp', 'outer')), may hold values from 1 to 3, as said below
- item_kind: int32 [2, 96], P(None, ('dp', 'outer')), may hold values from 0 to 1, as said below
- item_offset: int32 [2, 96], P(None, ('dp', 'outer')), may hold values from 0 to 1216, as said below
- cross_qkv: bfloat16 [3, 768, 768], P(None, ('dp', 'outer')), may hold values from -0.21875 to 0.21875
- cross_out: bfloat16 [768, 768], P(('dp', 'outer')), may hold values from -0.875 to 0.875
- cross_up: bfloat16 [768, 3072], P(('dp', 'outer')), may hold values from -0.21875 to 0.21875
- cross_down: bfloat16 [3072, 768], P(('dp', 'outer')), may hold values from -0.109375 to 0.109375
- self_qkv: bfloat16 [3, 768, 768], P(None, ('dp', 'outer')), may hold values from -0.21875 to 0.21875
- self_out: bfloat16 [768, 768], P(('dp', 'outer')), may hold values from -0.625 to 0.625
- self_up: bfloat16 [768, 3072], P(('dp', 'outer')), may hold values from -0.21875 to 0.21875
- self_down: bfloat16 [3072, 768], P(('dp', 'outer')), may hold values from -0.109375 to 0.109375
- norm_gain: bfloat16 [5, 768], P(None, ('dp', 'outer')), may hold values from 0.5 to 1.5
- norm_bias: bfloat16 [5, 768], P(None, ('dp', 'outer')), may hold values from -3 to 3
- up_bias: bfloat16 [2, 3072], P(None, ('dp', 'outer')), may hold values from -3 to 3
- down_bias: bfloat16 [2, 768], P(None, ('dp', 'outer')), may hold values from -3 to 3
Outputs:
- latents_out: bfloat16 [2, 96, 128, 768], P(None, ('dp', 'outer'))
- grad_latents: float32 [2, 96, 128, 768], P(None, ('dp', 'outer'))
- grad_tokens: float32 [2, 41472, 768], P(None, ('dp', 'outer'))
- grad_cross_qkv: float32 [3, 768, 768], P(None, ('dp', 'outer'))
- grad_cross_out: float32 [768, 768], P(('dp', 'outer'))
- grad_cross_up: float32 [768, 3072], P(('dp', 'outer'))
- grad_cross_down: float32 [3072, 768], P(('dp', 'outer'))
- grad_self_qkv: float32 [3, 768, 768], P(None, ('dp', 'outer'))
- grad_self_out: float32 [768, 768], P(('dp', 'outer'))
- grad_self_up: float32 [768, 3072], P(('dp', 'outer'))
- grad_self_down: float32 [3072, 768], P(('dp', 'outer'))
- grad_norm_gain: float32 [5, 768], P(None, ('dp', 'outer'))
- grad_norm_bias: float32 [5, 768], P(None, ('dp', 'outer'))
- grad_up_bias: float32 [2, 3072], P(None, ('dp', 'outer'))
- grad_down_bias: float32 [2, 768], P(None, ('dp', 'outer'))
The draws below stay inside these ranges and needn't reach their ends.
Inputs may be any that keep to these rules, and one draw needn't show every extreme that they name: `item_count`: items a device holds in one micro-batch. `item_kind`: 1 marks a video of 3 x 392 patches and 40 text tokens, 0 an image of 392 patches and 40 text tokens. A device's micro-batch holds either one video in slot 0 or only images; slots at or past the device's count hold 0. `item_offset`: items lie end to end from token row 0 in slot order; an unused slot's offset is the number of rows in use.
All inputs are finite; a program needn't handle non-finite values.
Results may differ from the reference program's by a relative error of at most 0.014.
Values may be sent and summed in bfloat16 or wider, within the bound.
No kernel may reach another device: no remote copies, remote signals or barrier semaphores. Data moves between devices by JAX's collectives and lax.ppermute only.
A program may use at most 320 MiB of HBM per device.

```python
import jax
import jax.numpy as jnp
from jax import lax

D = 768
HEADS = 12
HEAD = 64
FF = 3072
LAT = 128
SLOTS = 3
MICRO = 2
IMG_LEN = 432
VID_LEN = 1216
TOK_DEV = 1296
ITEMS = 96
TOKENS = 41472
N_DP = 16
N_OUTER = 2


def layout_pattern(key):
    device_total = ITEMS // SLOTS
    cell_total = MICRO * device_total
    pattern = jax.random.randint(jax.random.fold_in(key, 101), (cell_total,), 0, SLOTS + 1)
    shuffled = jax.random.permutation(jax.random.fold_in(key, 202), cell_total)
    pattern = pattern.at[shuffled[0]].set(SLOTS).at[shuffled[1]].set(0)
    return pattern.reshape(MICRO, device_total).astype(jnp.int32)


def draw_item_count(key, part):
    pattern = layout_pattern(key)
    return jnp.where(pattern == 0, 1, pattern).astype(jnp.int32)


def draw_item_kind(key, part):
    pattern = layout_pattern(key)
    slot_ids = jnp.arange(SLOTS, dtype=jnp.int32)
    kind_all = (pattern[:, :, None] == 0) & (slot_ids[None, None, :] == 0)
    return kind_all.astype(jnp.int32).reshape(MICRO, ITEMS)


def draw_item_offset(key, part):
    pattern = layout_pattern(key)[:, :, None]
    slot_ids = jnp.arange(SLOTS, dtype=jnp.int32)[None, None, :]
    video_case = jnp.where(slot_ids == 0, 0, VID_LEN)
    image_case = jnp.minimum(slot_ids, pattern) * IMG_LEN
    return jnp.where(pattern == 0, video_case, image_case).astype(jnp.int32).reshape(MICRO, ITEMS)


def block_scale(key, dims, cuts, least, largest):
    def one(axis_at, shards_of):
        steps = jax.random.uniform(jax.random.fold_in(jax.random.fold_in(key, 6), axis_at), (shards_of,), jnp.float32, least / len(cuts), largest / len(cuts))
        return jnp.repeat(jnp.exp(steps), dims[axis_at] // shards_of).reshape((-1,) + (1,) * (len(dims) - axis_at - 1))

    loudness = one(*cuts[0])
    for cut in cuts[1:]:
        loudness = loudness * one(*cut)
    return loudness


def noise(stream_key, extent, scale, most, pieces=(), kind=jnp.bfloat16):
    factor_of = block_scale(stream_key, extent, pieces, -0.22, 0.18) if pieces else 1.0
    result = jax.random.normal(stream_key, extent, jnp.float32) * scale * factor_of
    return jnp.minimum(jnp.maximum(result, -most), most).astype(kind)


def setup_inputs(seed: int = 0) -> dict:
    key_of = jax.random.split(jax.random.key(seed), 19)
    latents = noise(key_of[0], (MICRO, ITEMS, LAT, D), 1.0, 6.0, ((1, 32),))
    tokens = noise(key_of[1], (MICRO, TOKENS, D), 1.0, 6.0, ((1, 32),))
    cotangent = noise(key_of[2], (MICRO, ITEMS, LAT, D), 1.0, 6.0, ((1, 32),))
    item_count = draw_item_count(jax.random.fold_in(key_of[18], 71), 0)
    item_kind = draw_item_kind(jax.random.fold_in(key_of[18], 71), 0)
    item_offset = draw_item_offset(jax.random.fold_in(key_of[18], 71), 0)
    cross_qkv = noise(key_of[6], (3, D, D), D ** -0.5, 0.21875, ((1, 32),))
    cross_out = noise(key_of[7], (D, D), (D // 16) ** -0.5, 0.875, ((0, 32),))
    cross_up = noise(key_of[8], (D, FF), D ** -0.5, 0.21875, ((0, 32),))
    cross_down = noise(key_of[9], (FF, D), FF ** -0.5, 0.109375, ((0, 32),))
    self_qkv = noise(key_of[10], (3, D, D), D ** -0.5, 0.21875, ((1, 32),))
    self_out = noise(key_of[11], (D, D), (D // 8) ** -0.5, 0.625, ((0, 32),))
    self_up = noise(key_of[12], (D, FF), D ** -0.5, 0.21875, ((0, 32),))
    self_down = noise(key_of[13], (FF, D), FF ** -0.5, 0.109375, ((0, 32),))
    norm_gain = jnp.clip(1.0 + 0.1 * jax.random.normal(key_of[14], (5, D), jnp.float32), 0.5, 1.5).astype(jnp.bfloat16)
    norm_bias = noise(key_of[15], (5, D), 0.3, 3.0, ((1, 32),))
    up_bias = noise(key_of[16], (2, FF), 0.3, 3.0, ((1, 32),))
    down_bias = noise(key_of[17], (2, D), 0.3, 3.0, ((1, 32),))
    return {"latents": latents, "tokens": tokens, "cotangent": cotangent, "item_count": item_count, "item_kind": item_kind, "item_offset": item_offset, "cross_qkv": cross_qkv, "cross_out": cross_out, "cross_up": cross_up, "cross_down": cross_down, "self_qkv": self_qkv, "self_out": self_out, "self_up": self_up, "self_down": self_down, "norm_gain": norm_gain, "norm_bias": norm_bias, "up_bias": up_bias, "down_bias": down_bias}


EPSILON = 1e-05
NEG_FILL = -1e+30

@jax.custom_vjp
def low(v):
    return lax.optimization_barrier(v.astype(jnp.bfloat16)).astype(jnp.float32)

@jax.custom_vjp
def low_back(v):
    return v

def low_keep(v):
    return (low(v), None)

def low_pass(kept, grad):
    return (grad,)

def back_keep(v):
    return (v, None)

def back_low(kept, grad):
    return (low(grad),)
low.defvjp(low_keep, low_pass)
low_back.defvjp(back_keep, back_low)

def both_ways(values):
    return low(low_back(values))

def product(left, right):
    return jnp.dot(left, right, precision=lax.Precision.HIGHEST)

def layer_norm(values, scale_row, shift_row):
    center = values - lax.optimization_barrier(jnp.mean(values, axis=-1, keepdims=True))
    inverse = lax.rsqrt(lax.optimization_barrier(jnp.mean(center * center, axis=-1, keepdims=True)) + EPSILON)
    return center * inverse * scale_row + shift_row

def attend(queries, key_rows, value_rows, mask_rows):
    row_count = queries.shape[0]
    query_heads = queries.reshape(row_count, HEADS, HEAD)
    key_heads = key_rows.reshape(key_rows.shape[0], HEADS, HEAD)
    value_heads = value_rows.reshape(value_rows.shape[0], HEADS, HEAD)
    scores = jnp.einsum('rhd,khd->hrk', query_heads, key_heads, precision=lax.Precision.HIGHEST)
    scores = low_back(scores * HEAD ** (-0.5))
    if mask_rows is not None:
        scores = jnp.where(mask_rows[None], scores, NEG_FILL)
    probs_low = low(jax.nn.softmax(scores, axis=-1))
    mixture = jnp.einsum('hrk,khd->rhd', probs_low, value_heads, precision=lax.Precision.HIGHEST)
    return mixture.reshape(row_count, HEADS * HEAD)

def attend_plain(queries, key_rows, value_rows):
    return attend(queries, key_rows, value_rows, None)

def feed_forward(residual, scale_row, shift_row, w_up, b_up, w_down, b_down):
    inner_in = low(layer_norm(residual, scale_row, shift_row))
    pre_act = low_back(product(inner_in, w_up) + b_up)
    activated = low(jax.nn.gelu(pre_act, approximate=True))
    return low_back(product(activated, w_down) + b_down)

def block_forward(params, lat_block, tok_block, member, live_slot):
    cross_qkv, cross_out, cross_up, cross_down, self_qkv, self_out, self_up, self_down, norm_gain, norm_bias, up_bias, down_bias = params
    slot_count, latent_count, model_width = lat_block.shape
    token_rows = tok_block.shape[0]
    residual = lat_block.reshape(slot_count * latent_count, model_width)
    query_in = low(layer_norm(residual, norm_gain[0], norm_bias[0]))
    token_in = low(layer_norm(tok_block, norm_gain[1], norm_bias[1]))
    queries = both_ways(product(query_in, cross_qkv[0]))
    key_rows = both_ways(product(token_in, cross_qkv[1]))
    value_rows = both_ways(product(token_in, cross_qkv[2]))
    mask_rows = jnp.broadcast_to(member[:, None, :], (slot_count, latent_count, token_rows))
    mask_rows = mask_rows.reshape(slot_count * latent_count, token_rows)
    mixture = both_ways(attend(queries, key_rows, value_rows, mask_rows))
    live_rows = jnp.repeat(live_slot, latent_count)[:, None]
    residual = residual + live_rows * low_back(product(mixture, cross_out))
    residual = residual + feed_forward(residual, norm_gain[2], norm_bias[2], cross_up, up_bias[0], cross_down, down_bias[0])
    self_in = low(layer_norm(residual, norm_gain[3], norm_bias[3]))
    shape_three = (slot_count, latent_count, model_width)
    queries_two = both_ways(product(self_in, self_qkv[0])).reshape(shape_three)
    keys_two = both_ways(product(self_in, self_qkv[1])).reshape(shape_three)
    values_two = both_ways(product(self_in, self_qkv[2])).reshape(shape_three)
    mixture_two = jax.vmap(attend_plain)(queries_two, keys_two, values_two)
    mixture_two = both_ways(mixture_two.reshape(slot_count * latent_count, model_width))
    residual = residual + low_back(product(mixture_two, self_out))
    residual = residual + feed_forward(residual, norm_gain[4], norm_bias[4], self_up, up_bias[1], self_down, down_bias[1])
    return residual.reshape(shape_three)

def reference(latents, tokens, cotangent, item_count, item_kind, item_offset, cross_qkv, cross_out, cross_up, cross_down, self_qkv, self_out, self_up, self_down, norm_gain, norm_bias, up_bias, down_bias):
    device_total = N_DP * N_OUTER
    block_total = MICRO * device_total
    params = tuple((weight.astype(jnp.float32) for weight in (cross_qkv, cross_out, cross_up, cross_down, self_qkv, self_out, self_up, self_down, norm_gain, norm_bias, up_bias, down_bias)))
    lat_blocks = latents.reshape(block_total, SLOTS, LAT, D)
    tok_blocks = tokens.reshape(block_total, TOK_DEV, D)
    cot_blocks = cotangent.reshape(block_total, SLOTS, LAT, D)
    count_blocks = item_count.reshape(block_total)
    kind_blocks = item_kind.reshape(block_total, SLOTS)
    offset_blocks = item_offset.reshape(block_total, SLOTS)

    def one_block(carry, block):
        lat_one, tok_one, cot_one, count_one, kind_one, offset_one = block
        slot_ids = jnp.arange(SLOTS, dtype=jnp.int32)
        live_slot = slot_ids < count_one
        lengths = jnp.where(kind_one == 1, VID_LEN, IMG_LEN).astype(jnp.int32) * live_slot.astype(jnp.int32)
        positions = jnp.arange(TOK_DEV, dtype=jnp.int32)
        member = (positions[None, :] >= offset_one[:, None]) & (positions[None, :] < (offset_one + lengths)[:, None])
        live_float = live_slot.astype(jnp.float32)

        def forward(weights_all, lat_in, tok_in):
            return block_forward(weights_all, lat_in, tok_in, member, live_float)
        output, pullback = jax.vjp(forward, params, lat_one.astype(jnp.float32), tok_one.astype(jnp.float32))
        grad_params, grad_lat, grad_tok = pullback(cot_one.astype(jnp.float32))
        carry = jax.tree.map(jnp.add, carry, grad_params)
        return (carry, (output.astype(jnp.bfloat16), grad_lat, grad_tok))
    start_sums = jax.tree.map(jnp.zeros_like, params)
    totals, (outputs, grad_lat, grad_tok) = lax.scan(one_block, start_sums, (lat_blocks, tok_blocks, cot_blocks, count_blocks, kind_blocks, offset_blocks))
    return (outputs.reshape(MICRO, ITEMS, LAT, D), grad_lat.reshape(MICRO, ITEMS, LAT, D), grad_tok.reshape(MICRO, TOKENS, D), totals[0], totals[1], totals[2], totals[3], totals[4], totals[5], totals[6], totals[7], totals[8], totals[9], totals[10], totals[11])
```

```python
import functools
from functools import partial

import jax
import jax.numpy as jnp
from jax import lax
from jax.experimental import pallas as pl
from jax.experimental.pallas import tpu as pltpu
from jax.sharding import PartitionSpec as P

HEADS = 12
IMG_LEN = 432
VID_LEN = 1216
EPSILON = 1e-05
NEG_FILL = -1e30
AXES = ("dp", "outer")
f32 = jnp.float32
bf16 = jnp.bfloat16


class Plan:
    def __init__(self, n):
        self.n = n
        self.nz = n // 8
        self.half = n // 2

    def masks(self, core):
        out = []
        for r in range(self.half):
            z = r % self.nz
            a = (r // self.nz) % 2
            b = r // (2 * self.nz)
            first, second = (2, 4) if core == 0 else (4, 2)
            out.append(z * 8 + a * first + b * second)
        return out

    def perm_z(self, k):
        return [(i, i ^ (k * 8)) for i in range(self.n)]

    def perm_a(self):
        return [(i, i ^ (2 if i % 2 == 0 else 4)) for i in range(self.n)]

    def perm_b(self):
        return [(i, i ^ (4 if i % 2 == 0 else 2)) for i in range(self.n)]

    def perm_c(self):
        return [(i, i ^ 1) for i in range(self.n)]

    def tables(self):
        me = lax.axis_index(AXES).astype(jnp.int32)
        core = me % 2
        m0 = jnp.array(self.masks(0), jnp.int32)
        m1 = jnp.array(self.masks(1), jnp.int32)
        mine = jnp.where(core == 0, m0, m1)
        other = jnp.where(core == 0, m1, m0)
        return me ^ mine, (me ^ 1) ^ other


def shift(x, perm):
    return lax.ppermute(x, AXES, perm)


def gather_slots(plan, own):
    rows = own.shape[0]
    parts = [own] + [shift(own, plan.perm_z(k)) for k in range(1, plan.nz)]
    held = jnp.concatenate(parts, axis=0)
    held = jnp.concatenate([held, shift(held, plan.perm_a())], axis=0)
    held = jnp.concatenate([held, shift(held, plan.perm_b())], axis=0)
    other = shift(held, plan.perm_c())
    shape = (plan.half, rows, own.shape[1])
    return held.reshape(shape), other.reshape(shape)


def add_low(a, b):
    return (a.astype(f32) + b.astype(f32)).astype(bf16)


def scatter_slots(plan, keep, send):
    acc = add_low(keep, shift(send, plan.perm_c()))
    h = plan.half // 2
    acc = add_low(acc[:h], shift(acc[h:], plan.perm_b()))
    h = h // 2
    acc = add_low(acc[:h], shift(acc[h:], plan.perm_a()))
    total = acc[0].astype(f32)
    for k in range(1, plan.nz):
        total = total + shift(acc[k], plan.perm_z(k)).astype(f32)
    return total


def pack_shard(kind, shard, width):
    if kind == "rows":
        return shard
    if kind == "wide":
        k = shard.shape[1] // width
        return jnp.concatenate([shard[:, j * width : (j + 1) * width] for j in range(k)], axis=0)
    return shard.reshape(-1, width)


def unpack_shard(kind, packed, shape, width):
    if kind == "rows":
        return packed
    if kind == "wide":
        k = shape[1] // width
        r = shape[0]
        return jnp.concatenate([packed[j * r : (j + 1) * r] for j in range(k)], axis=1)
    return packed.reshape(shape)


def whole_shape(kind, shape, n):
    if kind == "stack":
        return (shape[0], shape[1] * n, shape[2])
    return (shape[0] * n, shape[1])


def block_spec(kind, shape, pick):
    if kind == "stack":
        return pl.BlockSpec(shape, lambda i, *t: (0, pick(i, *t), 0))
    return pl.BlockSpec(shape, lambda i, *t: (pick(i, *t), 0))


def assemble(plan, tables, mine, other, kinds, shapes):
    width = mine.shape[2]
    half, n = plan.half, plan.n
    dest = jnp.concatenate(tables)

    def body(dest_ref, a_ref, b_ref, *outs):
        step = pl.program_id(0)

        def put(src):
            at = 0
            for kind, shape, out in zip(kinds, shapes, outs):
                if kind == "rows":
                    out[...] = src[0, at : at + shape[0], :]
                    at += shape[0]
                elif kind == "wide":
                    for j in range(shape[1] // width):
                        out[:, j * width : (j + 1) * width] = src[0, at : at + shape[0], :]
                        at += shape[0]
                else:
                    for j in range(shape[0]):
                        out[j] = src[0, at : at + shape[1], :]
                        at += shape[1]

        @pl.when(step < half)
        def _():
            put(a_ref)

        @pl.when(step >= half)
        def _():
            put(b_ref)

    rows = mine.shape[1]
    grid_spec = pltpu.PrefetchScalarGridSpec(
        num_scalar_prefetch=1,
        grid=(n,),
        in_specs=[
            pl.BlockSpec((1, rows, width), lambda i, t: (jnp.minimum(i, half - 1), 0, 0)),
            pl.BlockSpec((1, rows, width), lambda i, t: (jnp.maximum(i - half, 0), 0, 0)),
        ],
        out_specs=[block_spec(k, s, lambda i, t: t[i]) for k, s in zip(kinds, shapes)],
    )
    nbytes = 4 * n * rows * width
    return pl.pallas_call(
        body,
        out_shape=[jax.ShapeDtypeStruct(whole_shape(k, s, n), bf16) for k, s in zip(kinds, shapes)],
        grid_spec=grid_spec,
        cost_estimate=pl.CostEstimate(flops=0, bytes_accessed=nbytes, transcendentals=0),
        name="assemble",
    )(dest, mine, other)


def split_grads(plan, tables, grads, kinds, shapes, width):
    half = plan.half
    both = jnp.concatenate(tables)
    count = len(kinds)

    def rows_of(kind, shape):
        n = 1
        for v in shape:
            n *= v
        return n // width

    rows = sum(rows_of(k, s) for k, s in zip(kinds, shapes))

    def body(t_ref, *refs):
        ins, outs = refs[: 2 * count], refs[2 * count :]
        for which in range(2):
            out = outs[which]
            at = 0
            for kind, shape, src in zip(kinds, shapes, ins[which * count : (which + 1) * count]):
                if kind == "rows":
                    out[0, at : at + shape[0], :] = src[...].astype(bf16)
                    at += shape[0]
                elif kind == "wide":
                    for j in range(shape[1] // width):
                        out[0, at : at + shape[0], :] = src[:, j * width : (j + 1) * width].astype(bf16)
                        at += shape[0]
                else:
                    for j in range(shape[0]):
                        out[0, at : at + shape[1], :] = src[j].astype(bf16)
                        at += shape[1]

    grid_spec = pltpu.PrefetchScalarGridSpec(
        num_scalar_prefetch=1,
        grid=(half,),
        in_specs=[block_spec(k, s, lambda i, t: t[i]) for k, s in zip(kinds, shapes)]
        + [block_spec(k, s, lambda i, t: t[half + i]) for k, s in zip(kinds, shapes)],
        out_specs=[pl.BlockSpec((1, rows, width), lambda i, t: (i, 0, 0))] * 2,
    )
    nbytes = 6 * plan.n * rows * width
    return pl.pallas_call(
        body,
        out_shape=[jax.ShapeDtypeStruct((half, rows, width), bf16)] * 2,
        grid_spec=grid_spec,
        cost_estimate=pl.CostEstimate(flops=0, bytes_accessed=nbytes, transcendentals=0),
        name="split",
    )(both, *grads, *grads)


def dense(left, right):
    return jnp.dot(left, right, preferred_element_type=f32)


def dense_back(grad_rows, weight):
    return lax.dot_general(grad_rows, weight, (((1,), (1,)), ((), ())), preferred_element_type=f32)


def weight_grad(inputs, grad_rows):
    return lax.dot_general(inputs, grad_rows, (((0,), (0,)), ((), ())), preferred_element_type=f32)


def norm_forward(values, scale_row, shift_row):
    center = values - jnp.mean(values, axis=-1, keepdims=True)
    inverse = lax.rsqrt(jnp.mean(center * center, axis=-1, keepdims=True) + EPSILON)
    normed = center * inverse
    return (normed * scale_row + shift_row, normed, inverse)


def norm_backward(grad_out, normed, inverse, scale_row):
    grad_scale = jnp.sum(grad_out * normed, axis=0)
    grad_shift = jnp.sum(grad_out, axis=0)
    scaled = grad_out * scale_row
    centered = (
        scaled
        - jnp.mean(scaled, axis=-1, keepdims=True)
        - normed * jnp.mean(scaled * normed, axis=-1, keepdims=True)
    )
    return (inverse * centered, grad_scale, grad_shift)


def heads_of(block, head_count):
    return block.reshape(block.shape[:-1] + (head_count, block.shape[-1] // head_count))


def part_scores(queries, keys, mask, head_count):
    q, k = heads_of(queries, head_count), heads_of(keys, head_count)
    factor = q.shape[-1] ** (-0.5)
    scores = jnp.einsum("gprhd,gpkhd->gphrk", q, k, preferred_element_type=f32) * factor
    if mask is not None:
        scores = jnp.where(mask[:, :, None, None, :], scores, NEG_FILL)
    return scores


def share(x, joint, op):
    if joint is None:
        return x
    return jnp.where(joint[:, None, None, None, None], op(x, axis=1, keepdims=True), x)


def attend_forward(queries, keys, values, mask, joint, head_count):
    scores = part_scores(queries, keys, mask, head_count)
    row_max = share(jnp.max(scores, axis=-1, keepdims=True), joint, jnp.max)
    exponent = jnp.exp(scores - row_max)
    row_total = share(jnp.sum(exponent, axis=-1, keepdims=True), joint, jnp.sum)
    probs_low = (exponent / row_total).astype(bf16)
    mixture = jnp.einsum("gphrk,gpkhd->gprhd", probs_low, heads_of(values, head_count), preferred_element_type=f32)
    return mixture.reshape(queries.shape), row_max + jnp.log(row_total)


def attend_backward(grad_mixture, queries, keys, values, mask, joint, log_total, head_count):
    scores = part_scores(queries, keys, mask, head_count)
    probs = jnp.exp(scores - log_total)
    grad_heads = heads_of(grad_mixture, head_count)
    grad_probs = jnp.einsum("gprhd,gpkhd->gphrk", grad_heads, heads_of(values, head_count), preferred_element_type=f32)
    grad_values = jnp.einsum("gphrk,gprhd->gpkhd", probs.astype(bf16), grad_heads, preferred_element_type=f32)
    inner = share(jnp.sum(probs * grad_probs, axis=-1, keepdims=True), joint, jnp.sum)
    grad_scores = (probs * (grad_probs - inner)).astype(bf16)
    factor = grad_heads.shape[-1] ** (-0.5)
    grad_query = jnp.einsum("gphrk,gpkhd->gprhd", grad_scores, heads_of(keys, head_count), preferred_element_type=f32) * factor
    grad_keys = jnp.einsum("gphrk,gprhd->gpkhd", grad_scores, heads_of(queries, head_count), preferred_element_type=f32) * factor
    return (
        grad_query.reshape(queries.shape),
        grad_keys.reshape(keys.shape).astype(bf16),
        grad_values.reshape(values.shape).astype(bf16),
    )


def feed_forward(residual, scale_row, shift_row, w_up, b_up, w_down, b_down):
    normed_out, normed, inverse = norm_forward(residual, scale_row, shift_row)
    inner_in = normed_out.astype(bf16)
    pre_act = dense(inner_in, w_up) + b_up
    activated = jax.nn.gelu(pre_act, approximate=True).astype(bf16)
    return (dense(activated, w_down) + b_down, (inner_in, pre_act, activated, normed, inverse))


def feed_backward(grad_out, saved, scale_row, w_up, w_down):
    inner_in, pre_act, activated, normed, inverse = saved
    grad_low = grad_out.astype(bf16)
    grad_down = weight_grad(activated, grad_low)
    grad_down_shift = jnp.sum(grad_low.astype(f32), axis=0)
    grad_act = dense_back(grad_low, w_down)
    unused, gelu_pull = jax.vjp(partial(jax.nn.gelu, approximate=True), pre_act)
    grad_pre = gelu_pull(grad_act)[0].astype(bf16)
    grad_up = weight_grad(inner_in, grad_pre)
    grad_up_shift = jnp.sum(grad_pre.astype(f32), axis=0)
    grad_in, grad_scale, grad_shift = norm_backward(dense_back(grad_pre, w_up), normed, inverse, scale_row)
    return (grad_in, (grad_up, grad_down, grad_up_shift, grad_down_shift, grad_scale, grad_shift))


class TreeExchange:
    def __init__(self, n, width):
        self.plan = Plan(n)
        self.width = width
        self.tables = self.plan.tables()
        self.last = None

    def gather(self, kinds, shards):
        width = self.width
        own = [pack_shard(k, s, width) for k, s in zip(kinds, shards)]
        own = jnp.concatenate(own, axis=0) if len(own) > 1 else own[0]
        if self.last is not None:
            own, unused = lax.optimization_barrier((own, self.last))
        plan = self.plan
        rows = own.shape[0]
        parts = [own] + [shift(own, plan.perm_z(k)) for k in range(1, plan.nz)]
        self.last = parts[-1]
        held = jnp.concatenate(parts, axis=0)
        held = jnp.concatenate([held, shift(held, plan.perm_a())], axis=0)
        held = jnp.concatenate([held, shift(held, plan.perm_b())], axis=0)
        other = shift(held, plan.perm_c())
        shape = (plan.half, rows, width)
        return assemble(plan, self.tables, held.reshape(shape), other.reshape(shape), kinds, [s.shape for s in shards])

    def scatter(self, kinds, grads, shapes):
        keep, send = split_grads(self.plan, self.tables, grads, kinds, shapes, self.width)
        total = scatter_slots(self.plan, keep, send)
        outs, at = [], 0
        for kind, shape in zip(kinds, shapes):
            size = 1
            for v in shape:
                size *= v
            rows = size // self.width
            outs.append(unpack_shard(kind, total[at : at + rows], shape, self.width))
            at += rows
        return outs


class PlainExchange:
    def __init__(self, n, width):
        self.n = n

    def gather(self, kinds, shards):
        return [lax.all_gather(s, AXES, axis=1 if k == "stack" else 0, tiled=True) for k, s in zip(kinds, shards)]

    def scatter(self, kinds, grads, shapes):
        return [
            lax.psum_scatter(g.astype(bf16), AXES, scatter_dimension=1 if k == "stack" else 0, tiled=True).astype(f32)
            for k, g in zip(kinds, grads)
        ]


SMALL_ROWS = 8


def pack_small(parts, width):
    flat = jnp.concatenate([p.reshape(-1) for p in parts])
    flat = jnp.pad(flat, (0, SMALL_ROWS * width - flat.shape[0]))
    return flat.reshape(SMALL_ROWS, width)


def spread_small(rows, n, shapes):
    flat = rows.reshape(n, -1)
    outs, at = [], 0
    for k, c in shapes:
        piece = flat[:, at : at + k * c].reshape(n, k, c)
        outs.append(piece.transpose(1, 0, 2).reshape(k, n * c))
        at += k * c
    return outs


def collect_small(wholes, n, width):
    pieces = [w.reshape(w.shape[0], n, -1).transpose(1, 0, 2).reshape(n, -1) for w in wholes]
    flat = jnp.concatenate(pieces, axis=1)
    flat = jnp.pad(flat, ((0, 0), (0, SMALL_ROWS * width - flat.shape[1])))
    return flat.reshape(n * SMALL_ROWS, width)


def part_small(rows, shapes):
    flat = rows.reshape(-1)
    outs, at = [], 0
    for k, c in shapes:
        outs.append(flat[at : at + k * c].reshape(k, c))
        at += k * c
    return outs


def local(
    latents,
    tokens,
    cotangent,
    item_count,
    item_kind,
    item_offset,
    cross_qkv,
    cross_out,
    cross_up,
    cross_down,
    self_qkv,
    self_out,
    self_up,
    self_down,
    norm_gain,
    norm_bias,
    up_bias,
    down_bias,
):
    micro, slots, lat, width = latents.shape
    token_rows = tokens.shape[1]
    rows = micro * slots * lat
    heads = HEADS
    n = lax.axis_size("dp") * lax.axis_size("outer")
    tree = n % 8 == 0 and n & (n - 1) == 0 and lax.axis_size("outer") == 2 and cross_out.shape[0] % 8 == 0
    link = TreeExchange(n, width) if tree else PlainExchange(n, width)

    small = [norm_gain, norm_bias, up_bias, down_bias]
    small_shapes = [s.shape for s in small]
    small_own = pack_small(small, width)
    small_rows, full_qkv = link.gather(["rows", "stack"], [small_own, cross_qkv])
    gains, shifts, up_shifts, down_shifts = spread_small(small_rows, n, small_shapes)
    full_out, full_up = link.gather(["rows", "wide"], [cross_out, cross_up])
    full_down, own_qkv = link.gather(["rows", "stack"], [cross_down, self_qkv])
    own_out, own_down = link.gather(["rows", "rows"], [self_out, self_down])
    (own_up,) = link.gather(["wide"], [self_up])

    live_slot = jnp.arange(slots, dtype=jnp.int32)[None] < item_count
    live_rows = jnp.repeat(live_slot.astype(f32).reshape(-1), lat)[:, None]
    video = item_kind[:, 0] == 1
    positions = jnp.arange(token_rows, dtype=jnp.int32).reshape(slots, -1)
    mask = jnp.logical_not(video)[:, None, None] | (positions < VID_LEN)[None]
    chunk = token_rows // slots
    shape_parts = (micro, slots, lat, width)

    def pick(x):
        x = x.reshape(shape_parts)
        return jnp.where(video[:, None, None, None], x[:, :1], x)

    def gathered(x):
        total = jnp.concatenate([jnp.sum(x, axis=1, keepdims=True), jnp.zeros_like(x[:, 1:])], axis=1)
        return jnp.where(video[:, None, None, None], total, x).astype(bf16).reshape(rows, width)

    residual = latents.reshape(rows, width).astype(f32)
    token_vals = tokens.reshape(micro * token_rows, width).astype(f32)
    query_out, query_normed, query_inv = norm_forward(residual, gains[0], shifts[0])
    query_in = query_out.astype(bf16)
    token_out, token_normed, token_inv = norm_forward(token_vals, gains[1], shifts[1])
    token_in = token_out.astype(bf16)
    queries = pick(dense(query_in, full_qkv[0]).astype(bf16))
    shape_keys = (micro, slots, chunk, width)
    key_rows = dense(token_in, full_qkv[1]).astype(bf16).reshape(shape_keys)
    value_rows = dense(token_in, full_qkv[2]).astype(bf16).reshape(shape_keys)
    cross_part, cross_log = attend_forward(queries, key_rows, value_rows, mask, video, heads)
    cross_mix = gathered(cross_part)
    resid_one = residual + live_rows * dense(cross_mix, full_out)
    ffn_one, saved_one = feed_forward(resid_one, gains[2], shifts[2], full_up, up_shifts[0], full_down, down_shifts[0])
    resid_two = resid_one + ffn_one
    self_out_rows, self_normed, self_inv = norm_forward(resid_two, gains[3], shifts[3])
    self_in = self_out_rows.astype(bf16)
    queries_two = dense(self_in, own_qkv[0]).astype(bf16).reshape(shape_parts)
    keys_two = dense(self_in, own_qkv[1]).astype(bf16).reshape(shape_parts)
    values_two = dense(self_in, own_qkv[2]).astype(bf16).reshape(shape_parts)
    self_mix, self_log = attend_forward(queries_two, keys_two, values_two, None, None, heads)
    self_mix = self_mix.astype(bf16).reshape(rows, width)
    resid_three = resid_two + dense(self_mix, own_out)
    ffn_two, saved_two = feed_forward(resid_three, gains[4], shifts[4], own_up, up_shifts[1], own_down, down_shifts[1])
    outputs = (resid_three + ffn_two).astype(bf16).reshape(latents.shape)

    grad_four = cotangent.reshape(rows, width).astype(f32)
    grad_in_two, ffn_two_grads = feed_backward(grad_four, saved_two, gains[4], own_up, own_down)
    owned_self_up, owned_self_down = link.scatter(
        ["wide", "rows"], list(ffn_two_grads[:2]), [self_up.shape, self_down.shape]
    )
    grad_three = grad_four + grad_in_two
    grad_attn_two = grad_three.astype(bf16)
    grad_self_out = weight_grad(self_mix, grad_attn_two)
    grad_mix_two = dense_back(grad_attn_two, own_out).astype(bf16).reshape(shape_parts)
    grad_q_two, grad_k_two, grad_v_two = attend_backward(
        grad_mix_two, queries_two, keys_two, values_two, None, None, self_log, heads
    )
    grad_q_two = grad_q_two.astype(bf16).reshape(rows, width)
    grad_k_two = grad_k_two.reshape(rows, width)
    grad_v_two = grad_v_two.reshape(rows, width)
    grad_self_qkv = jnp.stack(
        [weight_grad(self_in, grad_q_two), weight_grad(self_in, grad_k_two), weight_grad(self_in, grad_v_two)]
    )
    owned_self_qkv, owned_self_out = link.scatter(
        ["stack", "rows"], [grad_self_qkv, grad_self_out], [self_qkv.shape, self_out.shape]
    )
    grad_self_in = (
        dense_back(grad_q_two, own_qkv[0]) + dense_back(grad_k_two, own_qkv[1]) + dense_back(grad_v_two, own_qkv[2])
    )
    grad_norm_three, gain_three, shift_three = norm_backward(grad_self_in, self_normed, self_inv, gains[3])
    grad_two = grad_three + grad_norm_three
    grad_in_one, ffn_one_grads = feed_backward(grad_two, saved_one, gains[2], full_up, full_down)
    owned_cross_up, owned_cross_down = link.scatter(
        ["wide", "rows"], list(ffn_one_grads[:2]), [cross_up.shape, cross_down.shape]
    )
    grad_one = grad_two + grad_in_one
    grad_attn = (live_rows * grad_one).astype(bf16)
    grad_cross_out = weight_grad(cross_mix, grad_attn)
    grad_mix = pick(dense_back(grad_attn, full_out).astype(bf16))
    grad_query, grad_keys, grad_values = attend_backward(
        grad_mix, queries, key_rows, value_rows, mask, video, cross_log, heads
    )
    grad_query = gathered(grad_query)
    grad_keys = grad_keys.reshape(micro * token_rows, width)
    grad_values = grad_values.reshape(micro * token_rows, width)
    grad_cross_qkv = jnp.stack(
        [weight_grad(query_in, grad_query), weight_grad(token_in, grad_keys), weight_grad(token_in, grad_values)]
    )
    grad_lat_norm, gain_zero, shift_zero = norm_backward(
        dense_back(grad_query, full_qkv[0]), query_normed, query_inv, gains[0]
    )
    grad_tok_in = dense_back(grad_keys, full_qkv[1]) + dense_back(grad_values, full_qkv[2])
    grad_tok_rows, gain_first, shift_first = norm_backward(grad_tok_in, token_normed, token_inv, gains[1])
    grad_small = collect_small(
        [
            jnp.stack([gain_zero, gain_first, ffn_one_grads[4], gain_three, ffn_two_grads[4]]),
            jnp.stack([shift_zero, shift_first, ffn_one_grads[5], shift_three, ffn_two_grads[5]]),
            jnp.stack([ffn_one_grads[2], ffn_two_grads[2]]),
            jnp.stack([ffn_one_grads[3], ffn_two_grads[3]]),
        ],
        n,
        width,
    )
    owned_cross_qkv, owned_cross_out, owned_small = link.scatter(
        ["stack", "rows", "rows"],
        [grad_cross_qkv, grad_cross_out, grad_small],
        [cross_qkv.shape, cross_out.shape, small_own.shape],
    )
    owned_gain, owned_bias, owned_up_bias, owned_down_bias = part_small(owned_small, small_shapes)
    return (
        outputs,
        (grad_one + grad_lat_norm).reshape(latents.shape),
        grad_tok_rows.reshape(tokens.shape),
        owned_cross_qkv,
        owned_cross_out,
        owned_cross_up,
        owned_cross_down,
        owned_self_qkv,
        owned_self_out,
        owned_self_up,
        owned_self_down,
        owned_gain,
        owned_bias,
        owned_up_bias,
        owned_down_bias,
    )


def solution(mesh):
    both = ("dp", "outer")
    lane = P(None, both)
    stack = P(None, both, None)
    row = P(both, None)
    weights = (stack, row, row, row, stack, row, row, row, lane, lane, lane, lane)
    items = P(None, both, None, None)
    return jax.shard_map(
        local,
        mesh=mesh,
        in_specs=(items, stack, items, lane, lane, lane) + weights,
        out_specs=(items, items, stack) + weights,
        check_vma=False,
    )
```
